32 devices in a mesh: dp: 2 (over core), row: 4 (over z), col: 4 (over y, x).
Axes of the slice: x: 2, y: 2, z: 4, core: 2. Of those that a mesh axis runs over, the one named last changes fastest.
Arguments:
- tokens: bfloat16 [8192, 768], P(('dp', 'row'), 'col'), may hold values from -6.1 to 6.1
- prev_logits: bfloat16 [8, 12, 1024, 1024], P(('dp', 'row'), 'col'), may hold values from -6 to 6
- lengths: int32 [8], P(('dp', 'row')), may hold values from 513 to 1024, as said below
- w_query: bfloat16 [768, 768], P('row', 'col'), may hold values from -0.21875 to 0.21875
- b_query: float32 [768], P('col'), may hold values from -1.2 to 1.2
- w_key: bfloat16 [768, 768], P('row', 'col'), may hold values from -0.21875 to 0.21875
- w_value: bfloat16 [768, 768], P('row', 'col'), may hold values from -0.21875 to 0.21875
- b_value: float32 [768], P('col'), may hold values from -1.2 to 1.2
- w_out: bfloat16 [768, 768], P('col', 'row'), may hold values from -2 to 2
- b_out: float32 [768], P('col'), may hold values from -1.2 to 1.2
- gain_one: float32 [768], P('col'), may hold values from 0.5 to 1.5
- shift_one: float32 [768], P('col'), may hold values from -1.2 to 1.2
- w_up: bfloat16 [768, 3072], P('row', 'col'), may hold values from -0.21875 to 0.21875
- b_up: float32 [3072], P('col'), may hold values from -1.2 to 1.2
- w_down: bfloat16 [3072, 768], P('col', 'row'), may hold values from -0.109375 to 0.109375
- b_down: float32 [768], P('col'), may hold values from -1.2 to 1.2
- gain_two: float32 [768], P('col'), may hold values from 0.5 to 1.5
- shift_two: float32 [768], P('col'), may hold values from -1.2 to 1.2
- out_grad: bfloat16 [8192, 768], P(('dp', 'row'), 'col'), may hold values from -6 to 6
- logit_grad: bfloat16 [8, 12, 1024, 1024], P(('dp', 'row'), 'col'), may hold values from -1.1953125 to 1.1953125
Outputs:
- layer_out: bfloat16 [8192, 768], P(('dp', 'row'), 'col')
- new_logits: bfloat16 [8, 12, 1024, 1024], P(('dp', 'row'), 'col')
- tokens_grad: bfloat16 [8192, 768], P(('dp', 'row'), 'col')
- prev_grad: bfloat16 [8, 12, 1024, 1024], P(('dp', 'row'), 'col')
- grad_w_query: float32 [768, 768], P('row', 'col')
- grad_b_query: float32 [768], P('col')
- grad_w_key: float32 [768, 768], P('row', 'col')
- grad_w_value: float32 [768, 768], P('row', 'col')
- grad_b_value: float32 [768], P('col')
- grad_w_out: float32 [768, 768], P('col', 'row')
- grad_b_out: float32 [768], P('col')
- grad_gain_one: float32 [768], P('col')
- grad_shift_one: float32 [768], P('col')
- grad_w_up: float32 [768, 3072], P('row', 'col')
- grad_b_up: float32 [3072], P('col')
- grad_w_down: float32 [3072, 768], P('col', 'row')
- grad_b_down: float32 [768], P('col')
- grad_gain_two: float32 [768], P('col')
- grad_shift_two: float32 [768], P('col')
The draws below stay inside these ranges and needn't reach their ends.
Inputs may be any that keep to these rules, and one draw needn't show every extreme that they name: Slot s holds one sequence in its first lengths[s] positions; the rest is padding. Some slot is full.
All inputs are finite; a program needn't handle non-finite values.
Results may differ from the reference program's by a relative error of at most 0.012.
Values may be sent and summed in bfloat16 or wider, within the bound.
No kernel may reach another device: no remote copies, remote signals or barrier semaphores. Data moves between devices by JAX's collectives and lax.ppermute only.
A program may use at most 128 MiB of HBM per device.

```python
import math
import jax
import jax.numpy as jnp
from jax import lax

D = 768
H = 12
HD = 64
FF = 3072
SLOT = 1024
SLOTS = 8
TOKENS = 8192


def draw_tokens(key, part):
    column = jnp.arange(D, dtype=jnp.float32) / (D - 1)
    base_draw = jnp.clip(jax.random.normal(jax.random.fold_in(key, 7), (TOKENS, D), jnp.float32), -4.0, 4.0)
    factor = 0.5 + column
    return (base_draw * factor[None, :]).astype(jnp.bfloat16)


def draw_lengths(key, part):
    streams = jax.random.split(jax.random.fold_in(key, 5), 3)
    drawn_len = jax.random.randint(streams[0], (SLOTS,), SLOT // 2 + 1, SLOT + 1)
    full_at = jax.random.randint(streams[1], (), 0, SLOTS)
    short_at = (full_at + jax.random.randint(streams[2], (), 1, SLOTS)) % SLOTS
    position = jnp.arange(SLOTS)
    drawn_len = jnp.where(position == short_at, SLOT // 2 + 1, drawn_len)
    return jnp.where(position == full_at, SLOT, drawn_len).astype(jnp.int32)


def level_of(stream_key, dims, cuts, smallest, high):
    loudness = 1.0
    for axis_at, parts in cuts:
        draws = jax.random.uniform(jax.random.fold_in(jax.random.fold_in(stream_key, 6), axis_at), (parts,), jnp.float32, smallest / len(cuts), high / len(cuts))
        loudness = loudness * jnp.repeat(jnp.exp(draws), dims[axis_at] // parts).reshape((-1,) + (1,) * (len(dims) - 1 - axis_at))
    return loudness


def normal_values(rng, shape, deviation, reach, cuts=(), kind=jnp.bfloat16):
    factor_of = level_of(rng, shape, cuts, -0.22, 0.18) if cuts else 1.0
    result = jax.random.normal(rng, shape, jnp.float32) * deviation * factor_of
    return jnp.minimum(jnp.maximum(result, -reach), reach).astype(kind)


def setup_inputs(seed: int = 0) -> dict:
    key_list = jax.random.split(jax.random.key(seed), 21)
    tokens = draw_tokens(jax.random.fold_in(key_list[20], 71), 0)
    prev_logits = normal_values(key_list[1], (SLOTS, H, SLOT, SLOT), 1.0, 6.0, ((0, 8), (1, 4)))
    lengths = draw_lengths(jax.random.fold_in(key_list[20], 71), 0)
    w_query = normal_values(key_list[3], (D, D), D ** -0.5, 0.21875, ((0, 4), (1, 4)))
    b_query = normal_values(key_list[4], (D,), 0.2, 1.2, ((0, 4),), jnp.float32)
    w_key = normal_values(key_list[5], (D, D), D ** -0.5, 0.21875, ((0, 4), (1, 4)))
    w_value = normal_values(key_list[6], (D, D), D ** -0.5, 0.21875, ((0, 4), (1, 4)))
    b_value = normal_values(key_list[7], (D,), 0.2, 1.2, ((0, 4),), jnp.float32)
    w_out = normal_values(key_list[8], (D, D), (max(1, D * 10 // SLOT)) ** -0.5, 2.0, ((0, 4), (1, 4)))
    b_out = normal_values(key_list[9], (D,), 0.2, 1.2, ((0, 4),), jnp.float32)
    gain_one = jnp.clip(1.0 + 0.1 * jax.random.normal(key_list[10], (D,), jnp.float32), 0.5, 1.5)
    shift_one = normal_values(key_list[11], (D,), 0.2, 1.2, ((0, 4),), jnp.float32)
    w_up = normal_values(key_list[12], (D, FF), D ** -0.5, 0.21875, ((0, 4), (1, 4)))
    b_up = normal_values(key_list[13], (FF,), 0.2, 1.2, ((0, 4),), jnp.float32)
    w_down = normal_values(key_list[14], (FF, D), FF ** -0.5, 0.109375, ((0, 4), (1, 4)))
    b_down = normal_values(key_list[15], (D,), 0.2, 1.2, ((0, 4),), jnp.float32)
    gain_two = jnp.clip(1.0 + 0.1 * jax.random.normal(key_list[16], (D,), jnp.float32), 0.5, 1.5)
    shift_two = normal_values(key_list[17], (D,), 0.2, 1.2, ((0, 4),), jnp.float32)
    out_grad = normal_values(key_list[18], (TOKENS, D), 1.0, 6.0, ((0, 8), (1, 4)))
    logit_grad = normal_values(key_list[19], (SLOTS, H, SLOT, SLOT), 0.2, 1.1953125, ((0, 8), (1, 4)))
    return {"tokens": tokens, "prev_logits": prev_logits, "lengths": lengths, "w_query": w_query, "b_query": b_query, "w_key": w_key, "w_value": w_value, "b_value": b_value, "w_out": w_out, "b_out": b_out, "gain_one": gain_one, "shift_one": shift_one, "w_up": w_up, "b_up": b_up, "w_down": w_down, "b_down": b_down, "gain_two": gain_two, "shift_two": shift_two, "out_grad": out_grad, "logit_grad": logit_grad}


@jax.custom_vjp
def low(v):
    return lax.optimization_barrier(v.astype(jnp.bfloat16)).astype(jnp.float32)

@jax.custom_vjp
def low_back(v):
    return v

def low_keep(v):
    return (low(v), None)

def low_pass(kept, grad):
    return (grad,)

def back_keep(v):
    return (v, None)

def back_low(kept, grad):
    return (low(grad),)
low.defvjp(low_keep, low_pass)
low_back.defvjp(back_keep, back_low)
eps_norm = 1e-06
highest = lax.Precision.HIGHEST

def norm_rows(operand, norm_gain, norm_shift):
    row_mean = lax.optimization_barrier(jnp.mean(operand, axis=-1, keepdims=True))
    centred = operand - row_mean
    spread = lax.optimization_barrier(jnp.mean(centred * centred, axis=-1, keepdims=True))
    return centred * lax.rsqrt(spread + eps_norm) * norm_gain + norm_shift

def block_forward(inputs, previous, valid_rows, w_query, b_query, w_key, w_value, b_value, w_out, b_out, gain_one, shift_one, w_up, b_up, w_down, b_down, gain_two, shift_two):
    seq_len = inputs.shape[0]
    query_rows = low(low_back(jnp.dot(inputs, w_query, precision=highest) + b_query))
    key_rows = low(low_back(jnp.dot(inputs, w_key, precision=highest)))
    value_rows = low(low_back(jnp.dot(inputs, w_value, precision=highest) + b_value))
    query_rows = query_rows.reshape(seq_len, H, HD)
    key_rows = key_rows.reshape(seq_len, H, HD)
    value_rows = value_rows.reshape(seq_len, H, HD)
    raw_score = jnp.einsum('qhd,khd->hqk', query_rows, key_rows, precision=highest) * (1.0 / math.sqrt(HD)) + previous
    raw_score = low_back(raw_score)
    pair_mask = valid_rows[:, None] * valid_rows[None, :]
    logits = raw_score * pair_mask[None]
    masked = jnp.where(valid_rows[None, None, :] > 0, raw_score, -1e+30)
    attn_prob = jax.nn.softmax(masked, axis=-1)
    mixed_rows = jnp.einsum('hqk,khd->qhd', low(attn_prob), value_rows, precision=highest).reshape(seq_len, D)
    mixed_rows = low(low_back(mixed_rows))
    branch = low_back(jnp.dot(mixed_rows, w_out, precision=highest))
    first_norm = norm_rows(inputs + branch + b_out, gain_one, shift_one)
    inner_pre = low_back(jnp.dot(low(first_norm), w_up, precision=highest) + b_up)
    active = low(jax.nn.gelu(inner_pre, approximate=False))
    second = low_back(jnp.dot(active, w_down, precision=highest))
    layer_out = norm_rows(first_norm + second + b_down, gain_two, shift_two) * valid_rows[:, None]
    return (layer_out, logits)

def reference(tokens, prev_logits, lengths, w_query, b_query, w_key, w_value, b_value, w_out, b_out, gain_one, shift_one, w_up, b_up, w_down, b_down, gain_two, shift_two, out_grad, logit_grad):
    params = tuple((weight_arg.astype(jnp.float32) for weight_arg in (w_query, b_query, w_key, w_value, b_value, w_out, b_out, gain_one, shift_one, w_up, b_up, w_down, b_down, gain_two, shift_two)))
    positions = jnp.arange(SLOT)

    def one_slot(totals, slot_items):
        slot_tokens, slot_prev, slot_length, slot_grad, slot_logit_grad = slot_items
        valid_rows = (positions < slot_length).astype(jnp.float32)

        def forward(inputs, previous, *weights):
            return block_forward(inputs, previous, valid_rows, *weights)
        outputs, pullback = jax.vjp(forward, slot_tokens.astype(jnp.float32), slot_prev.astype(jnp.float32), *params)
        gradients = pullback((slot_grad.astype(jnp.float32), slot_logit_grad.astype(jnp.float32)))
        totals = tuple((running + gradient for running, gradient in zip(totals, gradients[2:])))
        return (totals, (outputs[0].astype(jnp.bfloat16), outputs[1].astype(jnp.bfloat16), gradients[0].astype(jnp.bfloat16), gradients[1].astype(jnp.bfloat16)))
    initial = tuple((jnp.zeros_like(weight_arg) for weight_arg in params))
    slot_inputs = (tokens.reshape(-1, SLOT, D), prev_logits, lengths, out_grad.reshape(-1, SLOT, D), logit_grad)
    sums, stacked = lax.scan(one_slot, initial, slot_inputs)
    layer_out = stacked[0].reshape(-1, D)
    tokens_grad = stacked[2].reshape(-1, D)
    return (layer_out, stacked[1], tokens_grad, stacked[3], sums[0], sums[1], sums[2], sums[3], sums[4], sums[5], sums[6], sums[7], sums[8], sums[9], sums[10], sums[11], sums[12], sums[13], sums[14])
```

```python
from functools import partial
import math

import jax
import jax.numpy as jnp
from jax import lax
from jax.sharding import PartitionSpec as P

D = 768
HD = 64
EPS = 1e-06
BF = jnp.bfloat16
F32 = jnp.float32


def dot_plain(left_mat, right_mat):
    return jnp.dot(left_mat, right_mat, preferred_element_type=F32)


def dot_rows(left_mat, right_mat):
    return lax.dot_general(left_mat, right_mat, (((0,), (0,)), ((), ())), preferred_element_type=F32)


def dot_cols(left_mat, right_mat):
    return lax.dot_general(left_mat, right_mat, (((1,), (1,)), ((), ())), preferred_element_type=F32)


def swap(operand, axis_name, size, bits):
    return lax.ppermute(operand, axis_name, [(i, i ^ bits) for i in range(size)])


def pick(stack, index):
    return lax.dynamic_index_in_dim(stack, index, 0, keepdims=False)


def reorder(stack, me):
    return jnp.stack([pick(stack, b ^ me) for b in range(stack.shape[0])])


def spread(operand, size):
    return [operand] + [swap(operand, "col", size, k) for k in range(1, size)]


def exchange(blocks, size):
    return [blocks[0]] + [swap(blocks[k], "col", size, k) for k in range(1, size)]


def gather_rows(block, nrow, row_at, dp_at):
    if nrow != 4:
        return lax.all_gather(block, "row", axis=0, tiled=True)
    half = block.shape[0] // 2
    mine = lax.dynamic_slice_in_dim(block, dp_at * half, half, 0)
    part = jnp.stack([mine] + [swap(mine, "row", 4, j) for j in range(1, 4)])
    other = swap(part, "dp", 2, 1)
    low = jnp.where(dp_at == 0, part, other)
    high = jnp.where(dp_at == 0, other, part)
    both = reorder(jnp.concatenate([low, high], axis=1), row_at)
    return both.reshape(-1, block.shape[1])


def reduce_rows(grad, nrow, row_at, dp_at):
    if nrow != 4:
        part = lax.psum_scatter(grad, "row", scatter_dimension=0, tiled=True)
        return lax.psum(part, "dp")
    n = grad.shape[1]
    half = grad.shape[0] // 8
    blocks = grad.reshape(4, 2, half, n)
    mine = lax.dynamic_index_in_dim(blocks, dp_at, 1, keepdims=False)
    give = lax.dynamic_index_in_dim(blocks, 1 - dp_at, 1, keepdims=False).astype(BF)
    mine = mine + swap(give, "dp", 2, 1).astype(F32)
    total = pick(mine, row_at)
    low = mine.astype(BF)
    for j in range(1, 4):
        total = total + swap(pick(low, row_at ^ j), "row", 4, j).astype(F32)
    other = swap(total, "dp", 2, 1)
    first = jnp.where(dp_at == 0, total, other)
    second = jnp.where(dp_at == 0, other, total)
    return jnp.concatenate([first, second], axis=0)


def sum_small(vec, nrow):
    if nrow != 4:
        return lax.psum(vec, ("dp", "row"))
    vec = vec + swap(vec, "dp", 2, 1)
    vec = vec + swap(vec, "row", 4, 1)
    return vec + swap(vec, "row", 4, 2)


def norm(operand, gain, shift):
    mean = jnp.mean(operand, axis=1, keepdims=True)
    centred = operand - mean
    inv = lax.rsqrt(jnp.mean(centred * centred, axis=1, keepdims=True) + EPS)
    hat = centred * inv
    return hat * gain + shift, hat, inv


def norm_back(upstream, hat, inv, gain):
    scaled = upstream * gain
    plain = jnp.mean(scaled, axis=1, keepdims=True)
    cross = jnp.mean(scaled * hat, axis=1, keepdims=True)
    result = inv * (scaled - plain - hat * cross)
    return result, jnp.sum(upstream * hat, axis=0), jnp.sum(upstream, axis=0)


def attention_forward(query, key, value, prev_logits, valid, key_live):
    seq_len = query.shape[0]
    heads = prev_logits.shape[1]
    split = lambda m: m.reshape(seq_len, heads, HD)
    raw = (
        jnp.einsum("qhd,khd->hqk", split(query), split(key), preferred_element_type=F32)
        * (1.0 / math.sqrt(HD))
        + prev_logits[0].astype(F32)
    )
    new_logits = (raw * (valid[:, None] * valid[None, :])[None]).astype(BF)[None]
    masked = jnp.where(key_live, raw, -1e30)
    top = jnp.max(masked, axis=-1, keepdims=True)
    shifted = jnp.exp(masked - top)
    prob = (shifted / jnp.sum(shifted, axis=-1, keepdims=True)).astype(BF)
    mixed = jnp.einsum("hqk,khd->qhd", prob, split(value), preferred_element_type=F32)
    return new_logits, prob, mixed.reshape(seq_len, -1).astype(BF)


def attention_backward(query, key, value, prob, mixed, d_mixed, logit_grad, valid):
    seq_len = query.shape[0]
    heads = prob.shape[0]
    split = lambda m: m.reshape(seq_len, heads, HD)
    scale = 1.0 / math.sqrt(HD)
    d_prob = jnp.einsum("qhd,khd->hqk", split(d_mixed), split(value), preferred_element_type=F32)
    row_dot = jnp.sum(split(d_mixed.astype(F32) * mixed.astype(F32)), axis=2).T[:, :, None]
    pair = (valid[:, None] * valid[None, :])[None]
    d_raw = (prob.astype(F32) * (d_prob - row_dot) + logit_grad[0].astype(F32) * pair).astype(BF)
    d_query = jnp.einsum("hqk,khd->qhd", d_raw, split(key), preferred_element_type=F32) * scale
    d_key = jnp.einsum("hqk,qhd->khd", d_raw, split(query), preferred_element_type=F32) * scale
    d_value = jnp.einsum("hqk,qhd->khd", prob, split(d_mixed), preferred_element_type=F32)
    flat = lambda m: m.reshape(seq_len, -1).astype(BF)
    return d_raw[None], flat(d_query), flat(d_key), flat(d_value)


def shards(
    ncol,
    nrow,
    tokens,
    prev_logits,
    lengths,
    w_query,
    b_query,
    w_key,
    w_value,
    b_value,
    w_out,
    b_out,
    gain_one,
    shift_one,
    w_up,
    b_up,
    w_down,
    b_down,
    gain_two,
    shift_two,
    out_grad,
    logit_grad,
):
    col_at = lax.axis_index("col")
    row_at = lax.axis_index("row")
    dp_at = lax.axis_index("dp")
    seq_len, width = tokens.shape
    own = seq_len // ncol
    hidden = w_up.shape[1]
    valid = (jnp.arange(seq_len) < lengths[0]).astype(F32)
    key_live = (valid > 0)[None, None, :]
    valid_own = lax.dynamic_slice_in_dim(valid, col_at * own, own)[:, None]

    tok = spread(tokens, ncol)
    w_qkv = gather_rows(jnp.concatenate([w_query, w_key, w_value], axis=1), nrow, row_at, dp_at)
    vectors = jnp.stack([b_out, gain_one, shift_one, b_down, gain_two, shift_two])
    vectors = reorder(jnp.stack(spread(vectors, ncol)), col_at)
    vectors = vectors.transpose(1, 0, 2).reshape(6, 1, D)
    v_b_out, v_gain_one, v_shift_one, v_b_down, v_gain_two, v_shift_two = vectors
    w_out_t = gather_rows(w_out.T, nrow, row_at, dp_at)
    out_parts = spread(w_out_t, ncol)
    w_up_full = gather_rows(w_up, nrow, row_at, dp_at)
    w_down_t = gather_rows(w_down.T, nrow, row_at, dp_at)
    grad_blocks = out_grad.reshape(ncol, own, width)
    grad_rows = exchange([pick(grad_blocks, col_at ^ k) for k in range(ncol)], ncol)
    grad_rows = reorder(jnp.stack(grad_rows), col_at).transpose(1, 0, 2).reshape(own, D)

    qkv_blocks = w_qkv.reshape(ncol, width, 3 * width)
    qkv_parts = [pick(qkv_blocks, col_at ^ k) for k in range(ncol)]
    wide_tok = jnp.concatenate(tok, axis=1)
    qkv = dot_plain(wide_tok, jnp.concatenate(qkv_parts, axis=0))
    query = (qkv[:, :width] + b_query).astype(BF)
    key = qkv[:, width : 2 * width].astype(BF)
    value = (qkv[:, 2 * width :] + b_value).astype(BF)

    new_logits, prob, mixed = attention_forward(query, key, value, prev_logits, valid, key_live)

    mixed_blocks = mixed.reshape(ncol, own, width)
    mixed_rows = exchange([pick(mixed_blocks, col_at ^ k) for k in range(ncol)], ncol)
    branch = sum(dot_cols(mixed_rows[k], out_parts[k]) for k in range(ncol))
    tok_rows = jnp.stack([lax.dynamic_slice_in_dim(t, col_at * own, own, 0) for t in tok])
    tok_rows = reorder(tok_rows, col_at).transpose(1, 0, 2).reshape(own, D)
    first, first_hat, first_inv = norm(
        tok_rows.astype(F32) + branch + v_b_out, v_gain_one, v_shift_one
    )
    wide_first = jnp.concatenate(spread(first.astype(BF), ncol), axis=0)
    inner = dot_plain(wide_first, w_up_full) + b_up
    active, gelu_pull = jax.vjp(partial(jax.nn.gelu, approximate=False), inner)
    active = active.astype(BF)
    second_parts = dot_cols(active, w_down_t).astype(BF).reshape(ncol, own, D)
    second = sum(p.astype(F32) for p in exchange(list(second_parts), ncol))
    second_norm, second_hat, second_inv = norm(
        first + second + v_b_down, v_gain_two, v_shift_two
    )
    out_rows = (second_norm * valid_own).astype(BF)
    upstream = grad_rows.astype(F32) * valid_own
    g_two, g_gain_two, g_shift_two = norm_back(upstream, second_hat, second_inv, v_gain_two)
    g_b_down = jnp.sum(g_two, axis=0)
    wide_second = jnp.concatenate(spread(g_two.astype(BF), ncol), axis=0)
    out_blocks = out_rows.reshape(own, ncol, width).transpose(1, 0, 2)
    out_back = exchange([pick(out_blocks, col_at ^ k) for k in range(ncol)], ncol)
    layer_out = reorder(jnp.stack(out_back), col_at).reshape(seq_len, width)

    d_inner = gelu_pull(dot_plain(wide_second, w_down_t))[0].astype(BF)
    first_parts = dot_cols(d_inner, w_up_full).astype(BF).reshape(ncol, own, D)
    g_first = g_two + sum(p.astype(F32) for p in exchange(list(first_parts), ncol))
    g_one, g_gain_one, g_shift_one = norm_back(g_first, first_hat, first_inv, v_gain_one)
    g_b_out = jnp.sum(g_one, axis=0)
    d_branch = g_one.astype(BF)
    mixed_back = exchange([dot_plain(d_branch, out_parts[k]).astype(BF) for k in range(ncol)], ncol)
    d_mixed = reorder(jnp.stack(mixed_back), col_at).reshape(seq_len, width)
    wide_branch = reorder(jnp.stack(spread(d_branch, ncol)), col_at).reshape(seq_len, D)

    grad_down_t = dot_rows(wide_second, active)
    grad_up = dot_rows(wide_first, d_inner)
    g_b_up = jnp.sum(d_inner.astype(F32), axis=0)
    sum_down_t = reduce_rows(grad_down_t, nrow, row_at, dp_at)
    sum_up = reduce_rows(grad_up, nrow, row_at, dp_at)
    grad_out_t = dot_rows(wide_branch, mixed)
    sum_out_t = reduce_rows(grad_out_t, nrow, row_at, dp_at)

    row_vecs = jnp.stack([g_b_out, g_gain_one, g_shift_one, g_b_down, g_gain_two, g_shift_two])
    row_vecs = row_vecs.reshape(6, ncol, width).transpose(1, 0, 2)
    row_vecs = sum(exchange([pick(row_vecs, col_at ^ k) for k in range(ncol)], ncol))
    small = jnp.concatenate([row_vecs, g_b_up.reshape(-1, width)], axis=0)
    small = sum_small(small, nrow)

    prev_grad, d_query, d_key, d_value = attention_backward(
        query, key, value, prob, mixed, d_mixed, logit_grad, valid
    )
    d_qkv = jnp.concatenate([d_query, d_key, d_value], axis=1)
    token_parts = [dot_cols(d_qkv, qkv_parts[k]).astype(BF) for k in range(ncol)]
    token_back = exchange(token_parts, ncol)
    g_cols = lax.dynamic_slice_in_dim(wide_branch, col_at * width, width, 1)
    tokens_grad = g_cols.astype(F32) + sum(p.astype(F32) for p in token_back)
    tokens_grad = tokens_grad.astype(BF)
    grad_qkv = dot_rows(wide_tok, d_qkv).reshape(ncol, width, 3 * width)
    grad_qkv = reorder(grad_qkv, col_at).reshape(D, 3 * width)
    sum_qkv = reduce_rows(grad_qkv, nrow, row_at, dp_at)
    head_small = jnp.sum(d_qkv.astype(F32), axis=0).reshape(3, width)
    head_small = sum_small(head_small, nrow)

    return (
        layer_out,
        new_logits,
        tokens_grad,
        prev_grad,
        sum_qkv[:, :width],
        head_small[0],
        sum_qkv[:, width : 2 * width],
        sum_qkv[:, 2 * width :],
        head_small[2],
        sum_out_t.T,
        small[0],
        small[1],
        small[2],
        sum_up,
        small[6:].reshape(hidden),
        sum_down_t.T,
        small[3],
        small[4],
        small[5],
    )


def solution(mesh):
    wide = P(("dp", "row"), "col")
    heads = P(("dp", "row"), "col", None, None)
    weight = P("row", "col")
    turned = P("col", "row")
    vec = P("col")
    in_specs = (
        wide, heads, P(("dp", "row")), weight, vec, weight, weight, vec, turned, vec, vec, vec,
        weight, vec, turned, vec, vec, vec, wide, heads,
    )
    out_specs = (
        wide, heads, wide, heads, weight, vec, weight, weight, vec, turned, vec, vec, vec,
        weight, vec, turned, vec, vec, vec,
    )
    body = partial(shards, mesh.shape["col"], mesh.shape["row"])
    return jax.shard_map(body, mesh=mesh, in_specs=in_specs, out_specs=out_specs, check_vma=False)
```

```python
from functools import partial
import math

import jax
import jax.numpy as jnp
from jax import lax
from jax.experimental import pallas as pl
from jax.experimental.pallas import tpu as pltpu
from jax.sharding import PartitionSpec as P

D = 768
HD = 64
EPS = 1e-06
BF = jnp.bfloat16
F32 = jnp.float32


def dot_plain(left_mat, right_mat):
    return jnp.dot(left_mat, right_mat, preferred_element_type=F32)


def dot_rows(left_mat, right_mat):
    return lax.dot_general(left_mat, right_mat, (((0,), (0,)), ((), ())), preferred_element_type=F32)


def dot_cols(left_mat, right_mat):
    return lax.dot_general(left_mat, right_mat, (((1,), (1,)), ((), ())), preferred_element_type=F32)


def swap(operand, axis_name, size, bits):
    return lax.ppermute(operand, axis_name, [(i, i ^ bits) for i in range(size)])


def pick(stack, index):
    return lax.dynamic_index_in_dim(stack, index, 0, keepdims=False)


def reorder(stack, me):
    return jnp.stack([pick(stack, b ^ me) for b in range(stack.shape[0])])


def spread(operand, size):
    return [operand] + [swap(operand, "col", size, k) for k in range(1, size)]


def exchange(blocks, size):
    return [blocks[0]] + [swap(blocks[k], "col", size, k) for k in range(1, size)]


def xor_rows(block, nrow):
    if nrow != 4:
        return lax.all_gather(block, "row", axis=0, tiled=True).reshape(4, -1, block.shape[1])
    return jnp.stack([block] + [swap(block, "row", 4, j) for j in range(1, 4)])


def halves(block, at):
    n = block.shape[1] // 2
    return [lax.dynamic_slice_in_dim(block, (at ^ s) * n, n, 1) for s in range(2)]


def qkv_kernel(order_ref, *refs):
    tok_refs, (w_ref, bias_ref, q_ref, k_ref, v_ref) = refs[:4], refs[4:]
    width = q_ref.shape[1]
    total = bias_ref[...]
    for k in range(4):
        total = total + dot_plain(tok_refs[k][...], w_ref[k ^ order_ref[0], :, : 3 * width])
    q_ref[...] = total[:, :width].astype(BF)
    k_ref[...] = total[:, width : 2 * width].astype(BF)
    v_ref[...] = total[:, 2 * width :].astype(BF)


def project(order, tok, weight, bias):
    rows, width = tok[0].shape
    step = 256
    piece = pl.BlockSpec((step, width), lambda i, o: (i, 0))
    return pl.pallas_call(
        qkv_kernel,
        out_shape=[jax.ShapeDtypeStruct((rows, width), BF)] * 3,
        grid_spec=pltpu.PrefetchScalarGridSpec(
            num_scalar_prefetch=1,
            grid=(rows // step,),
            in_specs=[piece] * 4
            + [
                pl.BlockSpec(weight.shape, lambda i, o: (0, 0, 0)),
                pl.BlockSpec(bias.shape, lambda i, o: (0, 0)),
            ],
            out_specs=[piece] * 3,
        ),
        name="project",
        cost_estimate=pl.CostEstimate(
            flops=2 * rows * 4 * width * 3 * width, bytes_accessed=4_000_000, transcendentals=0
        ),
    )(order, *tok, weight, bias)


STEP = 256
CHUNK = 16


def forward_kernel(len_ref, q_ref, k_ref, v_ref, prev_ref, new_ref, prob_ref, mixed_ref, s_ref):
    rows, seq_len = s_ref.shape
    base = pl.program_id(0) * rows
    count = len_ref[0]
    live = lax.broadcasted_iota(jnp.int32, (1, seq_len), 1) < count
    keep = jnp.where(live, 1.0, 0.0)
    bias = jnp.where(live, 0.0, -1e30)
    for h in range(prev_ref.shape[1]):
        cols = slice(h * HD, (h + 1) * HD)
        s_ref[...] = dot_cols(q_ref[:, cols] * BF(1.0 / math.sqrt(HD)), k_ref[:, cols])

        @pl.loop(0, rows // CHUNK, unroll=2)
        def _(c):
            at = pl.multiple_of(c * CHUNK, CHUNK)
            here = pl.ds(at, CHUNK)
            raw = s_ref[here, :] + prev_ref[0, h, here, :].astype(F32)
            row_id = lax.broadcasted_iota(jnp.int32, (CHUNK, 1), 0) + (base + at)
            row_keep = jnp.where(row_id < count, 1.0, 0.0)
            new_ref[0, h, here, :] = (raw * keep * row_keep).astype(BF)
            masked = raw + bias
            shifted = jnp.exp(masked - jnp.max(masked, axis=1, keepdims=True))
            inv = 1.0 / jnp.sum(shifted, axis=1, keepdims=True)
            prob_ref[h, here, :] = (shifted * inv).astype(BF)

        mixed_ref[:, cols] = dot_plain(prob_ref[h], v_ref[:, cols]).astype(BF)


def attend(lengths, query, key, value, prev_logits):
    seq_len, width = query.shape
    heads = prev_logits.shape[1]
    rows = pl.BlockSpec((STEP, width), lambda i, n: (i, 0))
    full = pl.BlockSpec((seq_len, width), lambda i, n: (0, 0))
    logits = pl.BlockSpec((1, heads, STEP, seq_len), lambda i, n: (0, 0, i, 0))
    probs = pl.BlockSpec((heads, STEP, seq_len), lambda i, n: (0, i, 0))
    return pl.pallas_call(
        forward_kernel,
        out_shape=[
            jax.ShapeDtypeStruct(prev_logits.shape, BF),
            jax.ShapeDtypeStruct(prev_logits.shape[1:], BF),
            jax.ShapeDtypeStruct((seq_len, width), BF),
        ],
        grid_spec=pltpu.PrefetchScalarGridSpec(
            num_scalar_prefetch=1,
            grid=(seq_len // STEP,),
            in_specs=[rows, full, full, logits],
            out_specs=[logits, probs, rows],
            scratch_shapes=[pltpu.VMEM((STEP, seq_len), F32)],
        ),
        name="attend",
        cost_estimate=pl.CostEstimate(
            flops=60_000_000_000, bytes_accessed=20_000_000, transcendentals=3_000_000
        ),
    )(lengths, query, key, value, prev_logits)


def backward_kernel(
    meta_ref, q_ref, k_ref, v_ref, mixed_ref, dmix_ref, prob_ref, lg_ref,
    draw_ref, dq_ref, dk_ref, dv_ref, s_ref, dk_acc, dv_acc, t_ref,
):
    rows, seq_len = s_ref.shape
    step = pl.program_id(0)
    base = step * rows
    count = meta_ref[0]
    live = lax.broadcasted_iota(jnp.int32, (1, seq_len), 1) < count
    keep = jnp.where(live, 1.0, 0.0)

    @pl.when(step == 0)
    def _():
        dk_acc[...] = jnp.zeros_like(dk_acc)
        dv_acc[...] = jnp.zeros_like(dv_acc)

    for h in range(prob_ref.shape[0]):
        cols = slice(h * HD, (h + 1) * HD)
        d_mixed = dmix_ref[0, :, cols]
        s_ref[...] = dot_cols(d_mixed, v_ref[:, cols])
        t_ref[...] = jnp.sum(
            d_mixed.astype(F32) * mixed_ref[:, cols].astype(F32), axis=1, keepdims=True
        )

        @pl.loop(0, rows // CHUNK, unroll=2)
        def _(c):
            at = pl.multiple_of(c * CHUNK, CHUNK)
            here = pl.ds(at, CHUNK)
            row_id = lax.broadcasted_iota(jnp.int32, (CHUNK, 1), 0) + (base + at)
            row_keep = jnp.where(row_id < count, 1.0, 0.0)
            prob = prob_ref[h, here, :].astype(F32)
            cotangent = lg_ref[0, h, here, :].astype(F32) * keep * row_keep
            d_raw = prob * (s_ref[here, :] - t_ref[here, :]) + cotangent
            draw_ref[0, h, here, :] = d_raw.astype(BF)

        d_raw = draw_ref[0, h]
        scale = 1.0 / math.sqrt(HD)
        dq_ref[:, cols] = (dot_plain(d_raw, k_ref[:, cols]) * scale).astype(BF)
        dk_acc[cols, :] += dot_rows(q_ref[:, cols], d_raw)
        dv_acc[cols, :] += dot_rows(d_mixed, prob_ref[h])

    @pl.when(step == pl.num_programs(0) - 1)
    def _():
        dk_ref[...] = (dk_acc[...] * (1.0 / math.sqrt(HD))).T.astype(BF)
        dv_ref[...] = dv_acc[...].T.astype(BF)


def attend_back(meta, query, key, value, mixed, d_mixed, prob, logit_grad):
    seq_len, width = query.shape
    heads = prob.shape[0]
    rows = pl.BlockSpec((STEP, width), lambda i, m: (i, 0))
    full = pl.BlockSpec((seq_len, width), lambda i, m: (0, 0))
    slot = pl.BlockSpec((1, STEP, width), lambda i, m: (i ^ m[1], 0, 0))
    logits = pl.BlockSpec((1, heads, STEP, seq_len), lambda i, m: (0, 0, i, 0))
    probs = pl.BlockSpec((heads, STEP, seq_len), lambda i, m: (0, i, 0))
    flat = jax.ShapeDtypeStruct((seq_len, width), BF)
    return pl.pallas_call(
        backward_kernel,
        out_shape=[jax.ShapeDtypeStruct(logit_grad.shape, BF), flat, flat, flat],
        grid_spec=pltpu.PrefetchScalarGridSpec(
            num_scalar_prefetch=1,
            grid=(seq_len // STEP,),
            in_specs=[rows, full, full, rows, slot, probs, logits],
            out_specs=[logits, rows, full, full],
            scratch_shapes=[
                pltpu.VMEM((STEP, seq_len), F32),
                pltpu.VMEM((width, seq_len), F32),
                pltpu.VMEM((width, seq_len), F32),
                pltpu.VMEM((STEP, 1), F32),
            ],
        ),
        name="attend_back",
        cost_estimate=pl.CostEstimate(
            flops=80_000_000_000, bytes_accessed=20_000_000, transcendentals=0
        ),
    )(meta, query, key, value, mixed, d_mixed, prob, logit_grad)


def widths(w_ref):
    half = w_ref.shape[2] // 2
    depth = w_ref.shape[0] * w_ref.shape[1]
    return (
        w_ref[:, :, :half].reshape(depth, half),
        w_ref[:, :, half:].reshape(depth, half),
    )


def ffn_kernel(x_ref, a_ref, b_ref, bias_ref, part_ref, active_ref, slope_ref):
    half = a_ref.shape[2] // 2
    total = None
    for s, w_ref in enumerate((a_ref, b_ref)):
        cols = slice(s * half, (s + 1) * half)
        up, down = widths(w_ref)
        inner = dot_plain(x_ref[...], up) + bias_ref[:, cols]
        phi = 0.5 + 0.5 * lax.erf(inner * math.sqrt(0.5))
        bell = jnp.exp(-0.5 * inner * inner) * (1.0 / math.sqrt(2.0 * math.pi))
        active = (inner * phi).astype(BF)
        active_ref[:, cols] = active
        slope_ref[:, cols] = (phi + inner * bell).astype(BF)
        term = dot_cols(active, down)
        total = term if total is None else total + term
    part_ref[...] = total.astype(BF)


def ffn(x, near, far, bias):
    rows = x.shape[0]
    hidden = bias.shape[1]
    wide = jax.ShapeDtypeStruct((rows, hidden), BF)
    return pl.pallas_call(
        ffn_kernel,
        out_shape=[jax.ShapeDtypeStruct(x.shape, BF), wide, wide],
        name="ffn",
        cost_estimate=pl.CostEstimate(
            flops=8_000_000_000, bytes_accessed=5_000_000, transcendentals=500_000
        ),
    )(x, near, far, bias)


def ffn_back_kernel(d_ref, a_ref, b_ref, slope_ref, part_ref, inner_ref):
    half = a_ref.shape[2] // 2
    total = None
    for s, w_ref in enumerate((a_ref, b_ref)):
        cols = slice(s * half, (s + 1) * half)
        up, down = widths(w_ref)
        d_inner = (dot_plain(d_ref[...], down) * slope_ref[:, cols].astype(F32)).astype(BF)
        inner_ref[:, cols] = d_inner
        term = dot_cols(d_inner, up)
        total = term if total is None else total + term
    part_ref[...] = total.astype(BF)


def ffn_back(d, near, far, slope):
    return pl.pallas_call(
        ffn_back_kernel,
        out_shape=[jax.ShapeDtypeStruct(d.shape, BF), jax.ShapeDtypeStruct(slope.shape, BF)],
        name="ffn_back",
        cost_estimate=pl.CostEstimate(
            flops=8_000_000_000, bytes_accessed=5_000_000, transcendentals=0
        ),
    )(d, near, far, slope)


def split3(x):
    high = lax.reduce_precision(x, 8, 7)
    rest = x - high
    mid = lax.reduce_precision(rest, 8, 7)
    return jnp.concatenate([high, mid, rest - mid], axis=0).astype(BF)


def sum_rows(keep, give, extra, nrow):
    a, n = keep.shape[1:]
    low = extra.astype(BF)
    got = swap(jnp.concatenate([give.reshape(-1, n).astype(BF), low]), "dp", 2, 1)
    mine = keep + got[: 4 * a].reshape(4, a, n).astype(F32)
    both = (low.astype(F32) + got[4 * a :].astype(F32)).astype(BF)
    sent = mine.astype(BF)
    pieces = [swap(jnp.concatenate([sent[j], both]), "row", 4, j) for j in range(1, 4)]
    total = mine[0] + sum(p[:a].astype(F32) for p in pieces)
    e1, e2, e3 = (p[a:].astype(F32) for p in pieces)
    small = (both.astype(F32) + e1) + (e2 + e3)
    other = swap(total, "dp", 2, 1)
    return total, other, small


def norm(operand, gain, shift):
    mean = jnp.mean(operand, axis=1, keepdims=True)
    centred = operand - mean
    inv = lax.rsqrt(jnp.mean(centred * centred, axis=1, keepdims=True) + EPS)
    hat = centred * inv
    return hat * gain + shift, hat, inv


def norm_back(upstream, hat, inv, gain):
    scaled = upstream * gain
    plain = jnp.mean(scaled, axis=1, keepdims=True)
    cross = jnp.mean(scaled * hat, axis=1, keepdims=True)
    result = inv * (scaled - plain - hat * cross)
    return result, jnp.sum(upstream * hat, axis=0), jnp.sum(upstream, axis=0)


def shards(
    ncol,
    nrow,
    tokens,
    prev_logits,
    lengths,
    w_query,
    b_query,
    w_key,
    w_value,
    b_value,
    w_out,
    b_out,
    gain_one,
    shift_one,
    w_up,
    b_up,
    w_down,
    b_down,
    gain_two,
    shift_two,
    out_grad,
    logit_grad,
):
    few = nrow == 4
    col_at = lax.axis_index("col")
    dp_at = lax.axis_index("dp") if few else 0
    row_at = lax.axis_index("row") if few else 0
    order = row_at ^ col_at
    seq_len, width = tokens.shape
    own = seq_len // ncol
    hidden = w_up.shape[1]
    valid_own = (jnp.arange(own) + col_at * own < lengths[0]).astype(F32)[:, None]

    tok = spread(tokens, ncol)
    w_first = xor_rows(jnp.concatenate([w_query, w_key, w_value, w_out.T], axis=1), nrow)
    up_near, up_far = halves(w_up, dp_at)
    down_near, down_far = halves(w_down.T, dp_at)
    near = xor_rows(jnp.concatenate([up_near, down_near], axis=1), nrow)
    if few:
        far = swap(near, "dp", 2, 1)
    else:
        far = xor_rows(jnp.concatenate([up_far, down_far], axis=1), nrow)
    b_up_slots = jnp.concatenate(halves(b_up[None], dp_at), axis=1)

    bias = jnp.concatenate([b_query, jnp.zeros_like(b_query), b_value])[None]
    query, key, value = project(order[None], tok, w_first, bias)

    vectors = split3(jnp.stack([b_out, gain_one, shift_one, b_down, gain_two, shift_two]))
    vectors = jnp.pad(vectors, ((0, 14), (0, 0)))
    w_out_t = w_first[:, :, 3 * width :].reshape(D, width)
    grad_blocks = out_grad.reshape(ncol, own, width)
    mail = [
        jnp.concatenate([w_out_t, pick(grad_blocks, col_at ^ k), vectors], axis=0)
        for k in range(ncol)
    ]
    mail = exchange(mail, ncol)
    out_parts = [m[:D] for m in mail]
    side = jnp.stack([m[D:] for m in mail])
    side = jnp.concatenate([pick(side, j ^ order) for j in range(ncol)], axis=1)
    grad_rows = side[:own]
    vectors = side[own : own + 18].astype(F32).reshape(3, 6, 1, D).sum(axis=0)
    v_b_out, v_gain_one, v_shift_one, v_b_down, v_gain_two, v_shift_two = vectors

    new_logits, prob, mixed = attend(lengths, query, key, value, prev_logits)

    mixed_blocks = mixed.reshape(ncol, own, width)
    mixed_rows = exchange([pick(mixed_blocks, col_at ^ k) for k in range(ncol)], ncol)
    branch = sum(dot_cols(mixed_rows[k], out_parts[k]) for k in range(ncol))
    tok_rows = jnp.stack([lax.dynamic_slice_in_dim(t, col_at * own, own, 0) for t in tok])
    tok_rows = jnp.concatenate([pick(tok_rows, j ^ order) for j in range(ncol)], axis=1)
    first, first_hat, first_inv = norm(
        tok_rows.astype(F32) + branch + v_b_out, v_gain_one, v_shift_one
    )
    firsts = spread(first.astype(BF), ncol)
    lifted = [ffn(x, near, far, b_up_slots) for x in firsts]
    second = sum(p.astype(F32) for p in exchange([t[0] for t in lifted], ncol))
    second_norm, second_hat, second_inv = norm(
        first + second + v_b_down, v_gain_two, v_shift_two
    )
    out_rows = (second_norm * valid_own).astype(BF)
    upstream = grad_rows.astype(F32) * valid_own
    g_two, g_gain_two, g_shift_two = norm_back(upstream, second_hat, second_inv, v_gain_two)
    g_b_down = jnp.sum(g_two, axis=0)
    seconds = spread(g_two.astype(BF), ncol)
    dropped = [ffn_back(d, near, far, t[2]) for d, t in zip(seconds, lifted)]
    g_first = g_two + sum(p.astype(F32) for p in exchange([t[0] for t in dropped], ncol))
    g_one, g_gain_one, g_shift_one = norm_back(g_first, first_hat, first_inv, v_gain_one)
    g_b_out = jnp.sum(g_one, axis=0)
    d_branch = g_one.astype(BF)
    mixed_back = exchange([dot_plain(d_branch, out_parts[k]).astype(BF) for k in range(ncol)], ncol)

    row_sums = jnp.stack([g_b_out, g_gain_one, g_shift_one, g_b_down, g_gain_two, g_shift_two])
    row_sums = jnp.pad(row_sums.astype(BF), ((0, 10), (0, width)))
    out_blocks = out_rows.reshape(own, ncol, width).transpose(1, 0, 2)
    mail = [
        jnp.concatenate(
            [jnp.concatenate([d_branch, pick(out_blocks, order ^ k)], axis=1), row_sums], axis=0
        )
        for k in range(ncol)
    ]
    mail = reorder(jnp.stack(exchange(mail, ncol)), col_at)
    wide_branch = mail[:, :own, :D].reshape(seq_len, D)
    layer_out = mail[:, :own, D:].reshape(seq_len, width)
    at = (order * width) if few else (col_at * width)
    row_sums = lax.dynamic_slice_in_dim(mail[:, own : own + 6].astype(F32).sum(axis=0), at, width, 1)

    meta = jnp.stack([lengths[0], col_at.astype(jnp.int32)])
    prev_grad, d_query, d_key, d_value = attend_back(
        meta, query, key, value, mixed, jnp.stack(mixed_back), prob, logit_grad
    )
    d_qkv = jnp.concatenate([d_query, d_key, d_value], axis=1)
    qkv_parts = [pick(w_first, k ^ order)[:, : 3 * width] for k in range(ncol)]
    token_back = exchange([dot_cols(d_qkv, w).astype(BF) for w in qkv_parts], ncol)
    g_cols = lax.dynamic_slice_in_dim(wide_branch, at, width, 1)
    tokens_grad = g_cols.astype(F32) + sum(p.astype(F32) for p in token_back)
    tokens_grad = tokens_grad.astype(BF)

    cat = lambda parts: jnp.concatenate(parts, axis=0)
    d_inner = cat([t[1] for t in dropped])
    grad_up = dot_rows(cat(firsts), d_inner).reshape(4, -1, hidden)
    grad_down = dot_rows(cat(seconds), cat([t[1] for t in lifted])).reshape(4, -1, hidden)
    grad_out = dot_rows(wide_branch, mixed).reshape(4, -1, width)
    grad_qkv = dot_rows(jnp.concatenate(tok, axis=1), d_qkv).reshape(4, -1, 3 * width)
    grad_qkv = reorder(grad_qkv, order)
    grad_head = jnp.concatenate([grad_qkv, grad_out], axis=2)
    g_b_up = jnp.sum(d_inner.astype(F32), axis=0).reshape(2, -1)
    g_b_up = jnp.concatenate([pick(g_b_up, dp_at ^ s) for s in range(2)]).reshape(-1, width)
    small = jnp.concatenate([row_sums, g_b_up, jnp.sum(d_qkv.astype(F32), axis=0).reshape(3, width)])
    if few:
        n = hidden // 2
        near_up, near_down = grad_up[:, :, :n], grad_down[:, :, :n]
        far_up, far_down = grad_up[:, :, n:], grad_down[:, :, n:]
        mine, other, _ = sum_rows(
            jnp.concatenate([near_up, near_down], axis=2),
            jnp.concatenate([far_up, far_down], axis=2),
            jnp.zeros((16, hidden), F32),
            nrow,
        )
        up_sum = jnp.concatenate(
            [jnp.where(dp_at == 0, mine, other)[:, :n], jnp.where(dp_at == 0, other, mine)[:, :n]], 1
        )
        down_sum = jnp.concatenate(
            [jnp.where(dp_at == 0, mine, other)[:, n:], jnp.where(dp_at == 0, other, mine)[:, n:]], 1
        )
        blocks = grad_head.reshape(4, 2, -1, 4 * width)
        extra = jnp.pad(small, ((0, 3), (0, 0))).reshape(4, 4 * width)
        mine, other, small = sum_rows(
            lax.dynamic_index_in_dim(blocks, dp_at, 1, keepdims=False),
            lax.dynamic_index_in_dim(blocks, 1 - dp_at, 1, keepdims=False),
            jnp.pad(extra, ((0, 12), (0, 0))),
            nrow,
        )
        small = small[:4].reshape(16, width)
        head_sum = jnp.concatenate(
            [jnp.where(dp_at == 0, mine, other), jnp.where(dp_at == 0, other, mine)], 0
        )
    else:
        scatter = lambda g: lax.psum(
            lax.psum_scatter(g.reshape(D, -1), "row", scatter_dimension=0, tiled=True), "dp"
        )
        up_sum, down_sum, head_sum = scatter(grad_up), scatter(grad_down), scatter(grad_head)
        small = lax.psum(small, ("dp", "row"))

    return (
        layer_out,
        new_logits,
        tokens_grad,
        prev_grad,
        head_sum[:, :width],
        small[10],
        head_sum[:, width : 2 * width],
        head_sum[:, 2 * width : 3 * width],
        small[12],
        head_sum[:, 3 * width :].T,
        small[0],
        small[1],
        small[2],
        up_sum,
        small[6:10].reshape(hidden),
        down_sum.T,
        small[3],
        small[4],
        small[5],
    )


def solution(mesh):
    wide = P(("dp", "row"), "col")
    heads = P(("dp", "row"), "col", None, None)
    weight = P("row", "col")
    turned = P("col", "row")
    vec = P("col")
    in_specs = (
        wide, heads, P(("dp", "row")), weight, vec, weight, weight, vec, turned, vec, vec, vec,
        weight, vec, turned, vec, vec, vec, wide, heads,
    )
    out_specs = (
        wide, heads, wide, heads, weight, vec, weight, weight, vec, turned, vec, vec, vec,
        weight, vec, turned, vec, vec, vec,
    )
    body = partial(shards, mesh.shape["col"], mesh.shape["row"])
    return jax.shard_map(body, mesh=mesh, in_specs=in_specs, out_specs=out_specs, check_vma=False)
```
